128 devices in a mesh: mp: 16 (over y, x), hidden: 8 (over z, core).
Axes of the slice: x: 4, y: 4, z: 4, core: 2. Of those that a mesh axis runs over, the one named last changes fastest.
Arguments:
- states: bfloat16 [512, 16384], P(None, 'mp'), may hold values from -6 to 6
- gate_codes: bfloat16 [16384, 26624], P('mp', 'hidden'), may hold values from -127 to 127, as said below
- gate_scales: float32 [128, 26624], P('mp', 'hidden'), may hold values from 7.8125e-05 to 0.000703125
- up_codes: bfloat16 [16384, 26624], P('mp', 'hidden'), may hold values from -127 to 127, as said below
- up_scales: float32 [128, 26624], P('mp', 'hidden'), may hold values from 7.8125e-05 to 0.000703125
- down_codes: bfloat16 [26624, 16384], P('hidden', 'mp'), may hold values from -127 to 127, as said below
- down_scales: float32 [208, 16384], P('hidden', 'mp'), may hold values from 1.2257258e-05 to 0.000110315326
Outputs:
- output: bfloat16 [512, 16384], P(None, 'mp')
The draws below stay inside these ranges and needn't reach their ends.
Inputs may be any that keep to these rules, and one draw needn't show every extreme that they name: `gate_codes`: whole numbers. `up_codes`: whole numbers. `down_codes`: whole numbers.
All inputs are finite; a program needn't handle non-finite values. Where the reference program divides by a largest or mean magnitude, that divisor is 1e-20 or more.
Results may differ from the reference program's by a relative error of at most 0.02.
Values may be sent and summed in bfloat16 or wider, within the bound.
No kernel may reach another device: no remote copies, remote signals or barrier semaphores. Data moves between devices by JAX's collectives and lax.ppermute only.
A program may use at most 128 MiB of HBM per device.

```python
import math
import jax
import jax.numpy as jnp

D = 16384
FF = 26624
BLOCK = 128
ROWS = 512
N_MP = 16
N_HIDDEN = 8


def draw_gate_codes(key, part):
    return jax.random.randint(jax.random.fold_in(key, 11), (D, FF), -127, 128).astype(jnp.float32).astype(jnp.bfloat16)


def draw_up_codes(key, part):
    return jax.random.randint(jax.random.fold_in(key, 23), (D, FF), -127, 128).astype(jnp.float32).astype(jnp.bfloat16)


def draw_down_codes(key, part):
    return jax.random.randint(jax.random.fold_in(key, 37), (FF, D), -127, 128).astype(jnp.float32).astype(jnp.bfloat16)


def steps_of(own_key, extent, shards, low, high):
    loudness, own = 1.0, jax.random.fold_in(own_key, 6)
    for dim, shards_of in shards:
        heights = jnp.exp(jax.random.uniform(jax.random.fold_in(own, dim), (shards_of,), jnp.float32, low / len(shards), high / len(shards)))
        loudness = loudness * jnp.repeat(heights, extent[dim] // shards_of).reshape([-1 if axis == dim else 1 for axis in range(len(extent))])
    return loudness


def centred(rng, dims, deviation, most, split=(), held_as=jnp.bfloat16):
    values = deviation * jax.random.normal(rng, dims, jnp.float32)
    if split:
        values = values * steps_of(rng, dims, split, -0.22, 0.18)
    return jnp.clip(values, -most, most).astype(held_as)


def setup_inputs(seed: int = 0) -> dict:
    arg_keys = jax.random.split(jax.random.key(seed), 8)
    states = centred(arg_keys[0], (ROWS, D), 1.0, 6.0, ((1, 16),))
    gate_codes = draw_gate_codes(jax.random.fold_in(arg_keys[7], 71), 0)
    gate_scales = jnp.clip(jnp.exp(math.log(0.000703125) - 2.1972246 * jax.random.uniform(arg_keys[2], (D // BLOCK, FF), jnp.float32) ** steps_of(arg_keys[2], (D // BLOCK, FF), ((0, 16), (1, 8)), -0.2, 0.2)), 7.812499825377017e-05, 0.000703125)
    up_codes = draw_up_codes(jax.random.fold_in(arg_keys[7], 71), 0)
    up_scales = jnp.clip(jnp.exp(math.log(0.000703125) - 2.1972246 * jax.random.uniform(arg_keys[4], (D // BLOCK, FF), jnp.float32) ** steps_of(arg_keys[4], (D // BLOCK, FF), ((0, 16), (1, 8)), -0.2, 0.2)), 7.812499825377017e-05, 0.000703125)
    down_codes = draw_down_codes(jax.random.fold_in(arg_keys[7], 71), 0)
    down_scales = jnp.clip(jnp.exp(math.log(0.000110315326) - 2.1972246 * jax.random.uniform(arg_keys[6], (FF // BLOCK, D), jnp.float32) ** steps_of(arg_keys[6], (FF // BLOCK, D), ((0, 8), (1, 16)), -0.2, 0.2)), 1.225725827680435e-05, 0.000110315326)
    return dict(states=states, gate_codes=gate_codes, gate_scales=gate_scales, up_codes=up_codes, up_scales=up_scales, down_codes=down_codes, down_scales=down_scales)


epsilon = 1e-6


def dequantize(quantized, scales):
    depth, columns = quantized.shape
    groups = scales.shape[0]
    blocks = quantized.astype(jnp.float32).reshape(groups, depth // groups, columns)
    return (blocks * scales.astype(jnp.float32)[:, None, :]).reshape(depth, columns).astype(jnp.bfloat16)


def encode(values):
    row_count, columns = values.shape
    blocks = values.reshape(row_count, columns // BLOCK, BLOCK)
    maxima = (jnp.max(jnp.abs(blocks), axis=-1) + epsilon).astype(jnp.bfloat16)
    factor = 127.0 / maxima.astype(jnp.float32)
    codes = (blocks * factor[..., None]).astype(jnp.bfloat16)
    return codes.reshape(row_count, columns), maxima


def decode(codes, maxima):
    row_count, columns = codes.shape
    blocks = codes.astype(jnp.float32).reshape(row_count, columns // BLOCK, BLOCK)
    step_size = maxima.astype(jnp.float32) / 127.0
    return (blocks * step_size[..., None]).reshape(row_count, columns)


def reference(states, gate_codes, gate_scales, up_codes, up_scales, down_codes, down_scales):
    piece = D // N_MP
    groups = piece // BLOCK
    gate_sum = jnp.zeros((ROWS, FF), jnp.float32)
    up_sum = jnp.zeros((ROWS, FF), jnp.float32)
    for source in range(N_MP):
        inputs = states[:, source * piece:(source + 1) * piece]
        gate_w = dequantize(gate_codes[source * piece:(source + 1) * piece], gate_scales[source * groups:(source + 1) * groups])
        gate_part = jnp.dot(inputs, gate_w, preferred_element_type=jnp.float32)
        gate_sum = gate_sum + decode(*encode(gate_part))
        up_w = dequantize(up_codes[source * piece:(source + 1) * piece], up_scales[source * groups:(source + 1) * groups])
        up_part = jnp.dot(inputs, up_w, preferred_element_type=jnp.float32)
        up_sum = up_sum + decode(*encode(up_part))
    swiglu = jax.nn.silu(gate_sum) * up_sum
    activation = decode(*encode(swiglu)).astype(jnp.bfloat16)
    width = FF // N_HIDDEN
    wgroups = width // BLOCK
    result = jnp.zeros((ROWS, D), jnp.float32)
    for owner in range(N_HIDDEN):
        down_w = dequantize(down_codes[owner * width:(owner + 1) * width], down_scales[owner * wgroups:(owner + 1) * wgroups])
        result = result + jnp.dot(activation[:, owner * width:(owner + 1) * width], down_w, preferred_element_type=jnp.float32)
    return (result + states.astype(jnp.float32)).astype(jnp.bfloat16)
```

```python
import jax
import jax.numpy as jnp
from jax import lax
from jax.sharding import Mesh, PartitionSpec as P

BLOCK = 128
SIDE = 4
PLANE = ("y", "x", "core")


def hop(array, which, shift):
    pairs = []
    for y in range(SIDE):
        for x in range(SIDE):
            for c in range(2):
                if (c + which) % 2 == 0:
                    to = (y, (x + shift) % SIDE)
                else:
                    to = ((y + shift) % SIDE, x)
                pairs.append(((y * SIDE + x) * 2 + c, (to[0] * SIDE + to[1]) * 2 + c))
    return lax.ppermute(array, PLANE, pairs)


def hop_z(array, shift):
    return lax.ppermute(array, "z", [(i, (i + shift) % SIDE) for i in range(SIDE)])


def other_core(array):
    return lax.ppermute(array, "core", [(0, 1), (1, 0)])


def dequantize(quantized, scales):
    depth, columns = quantized.shape
    groups = scales.shape[0]
    blocks = quantized.astype(jnp.float32).reshape(groups, depth // groups, columns)
    return (blocks * scales[:, None, :]).reshape(depth, columns).astype(jnp.bfloat16)


def total(*terms):
    out = terms[0].astype(jnp.float32)
    for t in terms[1:]:
        out = out + t.astype(jnp.float32)
    return out


def scattered(gates, ups, which):
    relay_up = hop(ups[2], which, 1)
    relay_gate = hop(gates[2], which, -1)
    own_gate = hop(gates[1], which, 1)
    own_up = hop(ups[3], which, -1)
    sum_up = hop(total(ups[1], relay_up).astype(jnp.bfloat16), which, 1)
    sum_gate = hop(total(gates[3], relay_gate).astype(jnp.bfloat16), which, -1)
    return total(gates[0], own_gate, sum_gate), total(ups[0], sum_up, own_up)


def gathered(own, which):
    half = own.shape[0] // 2
    ahead_top = hop(own[:half], which, -1)
    behind_low = hop(own[half:], which, 1)
    ahead_low = hop(own[half:], which, -1)
    behind_top = hop(own[:half], which, 1)
    far_top = hop(ahead_top, which, -1)
    far_low = hop(behind_low, which, 1)
    return [own, (ahead_top, ahead_low), (far_top, far_low), (behind_top, behind_low)]


def gathered_small(own, which):
    return [own, hop(own, which, -1), hop(own, which, 2), hop(own, which, 1)]


def body(states, gate_codes, gate_scales, up_codes, up_scales, down_codes, down_scales):
    rows, width = states.shape
    columns = gate_codes.shape[1]
    core = lax.axis_index("core")
    ix, iy, iz = lax.axis_index("x"), lax.axis_index("y"), lax.axis_index("z")
    first = jnp.where(core == 0, ix, iy)
    second = jnp.where(core == 0, iy, ix)
    piece = rows // (SIDE * SIDE)
    turned = states.reshape(SIDE, SIDE, piece, width)
    turned = lax.dynamic_slice_in_dim(jnp.concatenate([turned, turned[:3]], 0), first, SIDE, 0)
    turned = lax.dynamic_slice_in_dim(jnp.concatenate([turned, turned[:, :3]], 1), second, SIDE, 1)
    turned = turned.reshape(rows, width)

    gate_w = dequantize(gate_codes, gate_scales)
    up_w = dequantize(up_codes, up_scales)
    gate = jnp.dot(turned, gate_w, preferred_element_type=jnp.float32).astype(jnp.bfloat16)
    up = jnp.dot(turned, up_w, preferred_element_type=jnp.float32).astype(jnp.bfloat16)
    q = rows // SIDE
    gates = [gate[k * q : (k + 1) * q] for k in range(SIDE)]
    ups = [up[k * q : (k + 1) * q] for k in range(SIDE)]
    gate, up = scattered(gates, ups, 0)
    gate, up = gate.astype(jnp.bfloat16), up.astype(jnp.bfloat16)
    gates = [gate[k * piece : (k + 1) * piece] for k in range(SIDE)]
    ups = [up[k * piece : (k + 1) * piece] for k in range(SIDE)]
    gate, up = scattered(gates, ups, 1)
    act = (jax.nn.silu(gate) * up).astype(jnp.bfloat16)

    parts = gathered_small(act, 1)
    line = jnp.zeros((SIDE, piece, columns), jnp.bfloat16)
    for k, part in enumerate(parts):
        line = lax.dynamic_update_slice_in_dim(line, part[None], (second + k) % SIDE, 0)
    line = line.reshape(q, columns)
    parts = gathered(line, 0)
    full = jnp.zeros((SIDE, 2, q // 2, columns), jnp.bfloat16)
    full = lax.dynamic_update_slice(full, line.reshape(1, 2, q // 2, columns), (first, 0, 0, 0))
    for k in range(1, SIDE):
        for h in range(2):
            full = lax.dynamic_update_slice(full, parts[k][h][None, None], ((first + k) % SIDE, h, 0, 0))
    activation = full.reshape(rows, columns)

    down_w = dequantize(down_codes, down_scales)
    part = jnp.dot(activation, down_w, preferred_element_type=jnp.float32).astype(jnp.bfloat16)
    half = rows // 2
    share = half // SIDE
    mine = lax.dynamic_slice_in_dim(part, core * half, half, 0)
    theirs = other_core(lax.dynamic_slice_in_dim(part, (1 - core) * half, half, 0))
    both = total(mine, theirs).astype(jnp.bfloat16).reshape(SIDE, share, width)

    def for_z(k):
        return lax.dynamic_index_in_dim(both, (iz + k) % SIDE, 0, keepdims=False)

    mine = total(for_z(0), hop_z(for_z(1), 1), hop_z(for_z(3), -1), hop_z(for_z(2), 2))
    residual = lax.dynamic_slice_in_dim(states, core * half + iz * share, share, 0)
    done = (mine + residual.astype(jnp.float32)).astype(jnp.bfloat16)
    pieces = [done, hop_z(done, -1), hop_z(done, 2), hop_z(done, 1)]
    mine = jnp.zeros((SIDE, share, width), jnp.bfloat16)
    for k, p in enumerate(pieces):
        mine = lax.dynamic_update_slice_in_dim(mine, p[None], (iz + k) % SIDE, 0)
    mine = mine.reshape(half, width)
    theirs = other_core(mine)
    out = jnp.zeros((rows, width), jnp.bfloat16)
    out = lax.dynamic_update_slice_in_dim(out, mine, core * half, 0)
    return lax.dynamic_update_slice_in_dim(out, theirs, (1 - core) * half, 0)


def solution(mesh):
    grid = Mesh(mesh.devices.reshape(SIDE, SIDE, SIDE, 2), ("y", "x", "z", "core"))
    mp, hidden = ("y", "x"), ("z", "core")
    in_specs = (
        P(None, mp),
        P(mp, hidden),
        P(mp, hidden),
        P(mp, hidden),
        P(mp, hidden),
        P(hidden, mp),
        P(hidden, mp),
    )
    return jax.shard_map(body, mesh=grid, in_specs=in_specs, out_specs=P(None, mp), check_vma=False)
```

```python
import functools

import jax
import jax.numpy as jnp
from jax import lax
from jax.experimental import pallas as pl
from jax.experimental.pallas import tpu as pltpu
from jax.sharding import Mesh, PartitionSpec as P

BLOCK = 128
SIDE = 4
TILES = (512, 896, 896, 1024)
DOWN_TILE = 512
PARTS = ((0, 0, 1), (0, 1, 3), (1, 0, 1), (1, 1, 3), (2, 0, 2), (2, 2, 2), (3, 0, 1), (3, 1, 3))
PLANE = ("y", "x", "core")


def hop(array, which, shift):
    pairs = []
    for y in range(SIDE):
        for x in range(SIDE):
            for c in range(2):
                if (c + which) % 2 == 0:
                    to = (y, (x + shift) % SIDE)
                else:
                    to = ((y + shift) % SIDE, x)
                pairs.append(((y * SIDE + x) * 2 + c, (to[0] * SIDE + to[1]) * 2 + c))
    return lax.ppermute(array, PLANE, pairs)


def hop_z(array, shift):
    return lax.ppermute(array, "z", [(i, (i + shift) % SIDE) for i in range(SIDE)])


def other_core(array):
    return lax.ppermute(array, "core", [(0, 1), (1, 0)])


def total(*terms):
    out = terms[0].astype(jnp.float32)
    for t in terms[1:]:
        out = out + t.astype(jnp.float32)
    return out


def rounded(*terms):
    return total(*terms).astype(jnp.bfloat16)


def weights(codes, scales):
    depth, columns = codes.shape
    groups = depth // BLOCK
    blocks = codes.astype(jnp.float32).reshape(groups, BLOCK, columns)
    return (blocks * scales[:, None, :]).reshape(depth, columns).astype(jnp.bfloat16)


def up_kernel(piece, place, states, gate_codes, gate_scales, up_codes, up_scales, *rest):
    outs, (turned, code_buf, scale_buf, out_buf, row_sem, code_sem, scale_sem, out_sem) = rest[:5], rest[5:]
    columns = gate_codes.shape[1]
    own, low1, top3, plus, minus = outs
    q = SIDE * piece
    half = q // 2
    targets = (
        (own, 0, q),
        (plus, half, half),
        (low1, 0, half),
        (minus, 0, half),
        (plus, 0, half),
        (top3, 0, half),
        (minus, half, half),
    )
    tiles = []
    for width in TILES:
        tiles.append((sum(w for _, w in tiles), width))
    jobs = [(m, at, width) for at, width in tiles for m in range(2)]

    def copy_codes(n):
        m, at, width = jobs[n]
        source = (gate_codes, up_codes)[m]
        return pltpu.make_async_copy(
            source.at[:, pl.ds(at, width)], code_buf.at[m, :, pl.ds(at, width)], code_sem.at[n]
        )

    def copy_rows(k):
        block = lax.rem(place[0] + k // SIDE, SIDE) * SIDE + lax.rem(place[1] + k % SIDE, SIDE)
        start = pl.multiple_of(block * piece, piece)
        return pltpu.make_async_copy(
            states.at[pl.ds(start, piece), :], turned.at[pl.ds(k * piece, piece), :], row_sem.at[k]
        )

    def copy_out(n, t):
        m, at, width = jobs[n]
        ref, start, size = targets[t]
        row = sum(size for _, _, size in targets[:t])
        return pltpu.make_async_copy(
            out_buf.at[m, pl.ds(row, size), pl.ds(at, width)],
            ref.at[pl.ds(start, size), pl.ds(m * columns + at, width)],
            out_sem.at[n, t],
        )

    copy_scales = [
        pltpu.make_async_copy(ref, scale_buf.at[m], scale_sem.at[m]) for m, ref in enumerate((gate_scales, up_scales))
    ]
    for k in range(SIDE * SIDE):
        copy_rows(k).start()
    for copy in copy_scales:
        copy.start()
    for n in range(len(jobs)):
        copy_codes(n).start()
    for k in range(SIDE * SIDE):
        copy_rows(k).wait()
    for copy in copy_scales:
        copy.wait()
    for n, (m, at, width) in enumerate(jobs):
        copy_codes(n).wait()
        w = weights(code_buf[m, :, at : at + width], scale_buf[m, :, at : at + width])
        part = jnp.dot(turned[...], w, preferred_element_type=jnp.float32)
        out_buf[m, :, at : at + width] = part.astype(jnp.bfloat16)
        for t in range(len(targets)):
            copy_out(n, t).start()
    for n in range(len(jobs)):
        for t in range(len(targets)):
            copy_out(n, t).wait()


def partial_sums(place, states, gate_codes, gate_scales, up_codes, up_scales):
    rows, width = states.shape
    columns = gate_codes.shape[1]
    q = rows // SIDE
    anywhere = pl.BlockSpec(memory_space=pl.ANY)
    return pl.pallas_call(
        functools.partial(up_kernel, q // SIDE),
        out_shape=tuple(jax.ShapeDtypeStruct((n, 2 * columns), jnp.bfloat16) for n in (q, q // 2, q // 2, q, q)),
        in_specs=[pl.BlockSpec(memory_space=pltpu.SMEM)] + [anywhere] * 5,
        out_specs=(anywhere,) * 5,
        scratch_shapes=[
            pltpu.VMEM((rows, width), jnp.bfloat16),
            pltpu.VMEM((2, width, columns), jnp.bfloat16),
            pltpu.VMEM((2, *gate_scales.shape), jnp.float32),
            pltpu.VMEM((2, rows, columns), jnp.bfloat16),
            pltpu.SemaphoreType.DMA((SIDE * SIDE,)),
            pltpu.SemaphoreType.DMA((2 * len(TILES),)),
            pltpu.SemaphoreType.DMA((2,)),
            pltpu.SemaphoreType.DMA((2 * len(TILES), 7)),
        ],
        compiler_params=pltpu.CompilerParams(vmem_limit_bytes=60 * 1024 * 1024),
        cost_estimate=pl.CostEstimate(
            flops=4 * rows * width * columns,
            bytes_accessed=4 * width * columns + 4 * rows * columns,
            transcendentals=0,
        ),
        name="partial_sums",
    )(place, states, gate_codes, gate_scales, up_codes, up_scales)


def down_kernel(piece, place, *rest):
    parts, (codes, scales, mine, theirs, act) = rest[:8], rest[8:]
    for (a, b, count), part in zip(PARTS, parts):
        for k in range(count):
            block = lax.rem(place[0] + a, SIDE) * SIDE + lax.rem(place[1] + b + k, SIDE)
            swap = lax.rem(lax.div(block, 2 * SIDE) + place[3], 2)
            ahead = lax.rem(lax.div(lax.rem(block, 2 * SIDE), 2) + SIDE - place[2], SIDE)
            at = (swap * SIDE + ahead) * 2 + lax.rem(block, 2)
            act[pl.ds(pl.multiple_of(at * piece, piece), piece), :] = part[k * piece : (k + 1) * piece, :]
    width = codes.shape[1]
    half = act.shape[0] // 2
    for at in range(0, width, DOWN_TILE):
        tile = slice(at, at + DOWN_TILE)
        out = jnp.dot(act[...], weights(codes[:, tile], scales[:, tile]), preferred_element_type=jnp.float32)
        out = out.astype(jnp.bfloat16)
        theirs[:, :, tile] = out[half:].reshape(SIDE, half // SIDE, DOWN_TILE)
        mine[:, :, tile] = out[:half].reshape(SIDE, half // SIDE, DOWN_TILE)


def down_sums(place, parts, codes, scales):
    depth, width = codes.shape
    rows = sum(p.shape[0] for p in parts)
    piece = rows // (SIDE * SIDE)
    vmem = pl.BlockSpec(memory_space=pltpu.VMEM)
    shape = jax.ShapeDtypeStruct((SIDE, rows // 2 // SIDE, width), jnp.bfloat16)
    return pl.pallas_call(
        functools.partial(down_kernel, piece),
        out_shape=(shape, shape),
        in_specs=[pl.BlockSpec(memory_space=pltpu.SMEM)] + [vmem] * 10,
        out_specs=(vmem, vmem),
        scratch_shapes=[pltpu.VMEM((rows, depth), jnp.bfloat16)],
        compiler_params=pltpu.CompilerParams(vmem_limit_bytes=24 * 1024 * 1024),
        cost_estimate=pl.CostEstimate(
            flops=2 * rows * depth * width, bytes_accessed=2 * (depth * width + rows * depth), transcendentals=0
        ),
        name="down_sums",
    )(place, *parts, codes, scales)


def sent_along_first(parts):
    own, low1, top3, plus, minus = parts
    half = own.shape[0] // 2
    plus = hop(plus, 0, 1)
    minus = hop(minus, 0, -1)
    sum_low = hop(rounded(low1, plus[:half]), 0, 1)
    sum_top = hop(rounded(top3, minus[:half]), 0, -1)
    top = rounded(own[:half], plus[half:], sum_top)
    low = rounded(own[half:], sum_low, minus[half:])
    piece = half // 2
    return top[:piece], top[piece:], low[:piece], low[piece:]


def sent_along_second(parts):
    return total(parts[0], hop(parts[1], 1, 1), hop(parts[3], 1, -1), hop(parts[2], 1, 2))


def body(states, gate_codes, gate_scales, up_codes, up_scales, down_codes, down_scales):
    rows, width = states.shape
    columns = gate_codes.shape[1]
    core = lax.axis_index("core")
    ix, iy, iz = lax.axis_index("x"), lax.axis_index("y"), lax.axis_index("z")
    first = jnp.where(core == 0, ix, iy)
    second = jnp.where(core == 0, iy, ix)
    place = jnp.stack([first, second, iz, core]).astype(jnp.int32)
    piece = rows // (SIDE * SIDE)

    parts = partial_sums(place, states, gate_codes, gate_scales, up_codes, up_scales)
    both = sent_along_second(sent_along_first(parts))
    gate, up = both[:, :columns], both[:, columns:]
    act = (jax.nn.silu(gate) * up).astype(jnp.bfloat16)

    side = jnp.concatenate([hop(act, 1, -1), hop(act, 1, 2), hop(act, 1, 1)], 0)
    ahead, behind = hop(act, 0, -1), hop(act, 0, 1)
    ahead_side, behind_side = hop(side, 0, -1), hop(side, 0, 1)
    ahead, behind, ahead_side, behind_side = lax.optimization_barrier((ahead, behind, ahead_side, behind_side))
    far01 = hop(jnp.concatenate([ahead, ahead_side[:piece]], 0), 0, -1)
    far23 = hop(behind_side[piece:], 0, 1)
    parts = (act, side, ahead, ahead_side, far01, far23, behind, behind_side)

    mine, theirs = down_sums(place, parts, down_codes, down_scales)
    both = rounded(mine, other_core(theirs))
    half = rows // 2
    share = half // SIDE
    got = total(both[0], hop_z(both[1], 1), hop_z(both[3], -1), hop_z(both[2], 2))
    residual = lax.dynamic_slice_in_dim(states, core * half + iz * share, share, 0)
    done = rounded(got, residual)
    mine = jnp.stack([done, hop_z(done, -1), hop_z(done, 2), hop_z(done, 1)])
    theirs = other_core(mine)
    out = jnp.zeros((2, SIDE, share, width), jnp.bfloat16)
    for k in range(SIDE):
        out = lax.dynamic_update_slice(out, mine[k][None, None], (core, (iz + k) % SIDE, 0, 0))
    for k in range(SIDE):
        out = lax.dynamic_update_slice(out, theirs[k][None, None], (1 - core, (iz + k) % SIDE, 0, 0))
    return out.reshape(rows, width)


def solution(mesh):
    grid = Mesh(mesh.devices.reshape(SIDE, SIDE, SIDE, 2), ("y", "x", "z", "core"))
    mp, hidden = ("y", "x"), ("z", "core")
    in_specs = (
        P(None, mp),
        P(mp, hidden),
        P(mp, hidden),
        P(mp, hidden),
        P(mp, hidden),
        P(hidden, mp),
        P(hidden, mp),
    )
    return jax.shard_map(body, mesh=grid, in_specs=in_specs, out_specs=P(None, mp), check_vma=False)
```

```python
import functools

import jax
import jax.numpy as jnp
from jax import lax
from jax.experimental import pallas as pl
from jax.experimental.pallas import tpu as pltpu
from jax.sharding import Mesh, PartitionSpec as P

BLOCK = 128
SIDE = 4
TILES = (512, 896, 896, 1024)
DEPTH = 2
DOWN_TILE = 512
PARTS = ((0, 0, 4), (1, 0, 4), (2, 0, 4), (3, 0, 4))
PLANE = ("y", "x", "core")


def hop(array, which, shift):
    pairs = []
    for y in range(SIDE):
        for x in range(SIDE):
            for c in range(2):
                if (c + which) % 2 == 0:
                    to = (y, (x + shift) % SIDE)
                else:
                    to = ((y + shift) % SIDE, x)
                pairs.append(((y * SIDE + x) * 2 + c, (to[0] * SIDE + to[1]) * 2 + c))
    return lax.ppermute(array, PLANE, pairs)


def hop_z(array, shift):
    return lax.ppermute(array, "z", [(i, (i + shift) % SIDE) for i in range(SIDE)])


def other_core(array):
    return lax.ppermute(array, "core", [(0, 1), (1, 0)])


def total(*terms):
    out = terms[0].astype(jnp.float32)
    for t in terms[1:]:
        out = out + t.astype(jnp.float32)
    return out


def rounded(*terms):
    return total(*terms).astype(jnp.bfloat16)


def weights(codes, scales):
    depth, columns = codes.shape
    groups = depth // BLOCK
    blocks = codes.astype(jnp.float32).reshape(groups, BLOCK, columns)
    return (blocks * scales[:, None, :]).reshape(depth, columns).astype(jnp.bfloat16)


def places():
    x, y, z, core = (lax.axis_index(name) for name in ("x", "y", "z", "core"))
    return jnp.where(core == 0, x, y), jnp.where(core == 0, y, x), z, core


def up_kernel(piece, halves, ends, states, gate_codes, gate_scales, up_codes, up_scales, *rest):
    outs, rest = rest[: len(ends)], rest[len(ends) :]
    turned, code_buf, scale_buf, out_buf, row_sem, code_sem, scale_sem, out_sem = rest
    place = places()
    columns = gate_codes.shape[1]
    size = 2 * piece
    tiles = []
    for width in TILES:
        tiles.append((sum(w for _, w in tiles), width))
    jobs = [(m, at, width) for at, width in tiles for m in range(2)]
    blocks = [(a, 2 * h + k) for a, h in halves for k in range(2)]

    def copy_codes(n):
        m, at, width = jobs[n]
        source = (gate_codes, up_codes)[m]
        return pltpu.make_async_copy(
            source.at[:, pl.ds(at, width)], code_buf.at[m, :, pl.ds(at, width)], code_sem.at[n]
        )

    def copy_rows(k):
        a, b = blocks[k]
        block = lax.rem(place[0] + a, SIDE) * SIDE + lax.rem(place[1] + b, SIDE)
        start = pl.multiple_of(block * piece, piece)
        return pltpu.make_async_copy(
            states.at[pl.ds(start, piece), :], turned.at[pl.ds(k * piece, piece), :], row_sem.at[k]
        )

    def copy_out(n, t):
        m, at, width = jobs[n]
        row = sum(ends[:t])
        return pltpu.make_async_copy(
            out_buf.at[m, pl.ds(row * size, ends[t] * size), pl.ds(at, width)],
            outs[t].at[:, pl.ds(m * columns + at, width)],
            out_sem.at[n, t],
        )

    copy_scales = [
        pltpu.make_async_copy(ref, scale_buf.at[m], scale_sem.at[m]) for m, ref in enumerate((gate_scales, up_scales))
    ]
    for k in range(len(blocks)):
        copy_rows(k).start()
    for copy in copy_scales:
        copy.start()
    for n in range(DEPTH):
        copy_codes(n).start()
    for k in range(len(blocks)):
        copy_rows(k).wait()
    for copy in copy_scales:
        copy.wait()
    for n, (m, at, width) in enumerate(jobs):
        copy_codes(n).wait()
        if n + DEPTH < len(jobs):
            copy_codes(n + DEPTH).start()
        w = weights(code_buf[m, :, at : at + width], scale_buf[m, :, at : at + width])
        part = jnp.dot(turned[...], w, preferred_element_type=jnp.float32)
        out_buf[m, :, at : at + width] = part.astype(jnp.bfloat16)
        for t in range(len(ends)):
            copy_out(n, t).start()
    for n in range(len(jobs)):
        for t in range(len(ends)):
            copy_out(n, t).wait()


def partial_sums(halves, ends, states, gate_codes, gate_scales, up_codes, up_scales):
    width = states.shape[1]
    columns = gate_codes.shape[1]
    piece = states.shape[0] // (SIDE * SIDE)
    rows = 2 * piece * len(halves)
    anywhere = pl.BlockSpec(memory_space=pl.ANY)
    return pl.pallas_call(
        functools.partial(up_kernel, piece, halves, ends),
        out_shape=tuple(jax.ShapeDtypeStruct((2 * piece * n, 2 * columns), jnp.bfloat16) for n in ends),
        in_specs=[anywhere] * 5,
        out_specs=(anywhere,) * len(ends),
        scratch_shapes=[
            pltpu.VMEM((rows, width), jnp.bfloat16),
            pltpu.VMEM((2, width, columns), jnp.bfloat16),
            pltpu.VMEM((2, *gate_scales.shape), jnp.float32),
            pltpu.VMEM((2, rows, columns), jnp.bfloat16),
            pltpu.SemaphoreType.DMA((2 * len(halves),)),
            pltpu.SemaphoreType.DMA((2 * len(TILES),)),
            pltpu.SemaphoreType.DMA((2,)),
            pltpu.SemaphoreType.DMA((2 * len(TILES), len(ends))),
        ],
        compiler_params=pltpu.CompilerParams(vmem_limit_bytes=60 * 1024 * 1024),
        cost_estimate=pl.CostEstimate(
            flops=4 * rows * width * columns,
            bytes_accessed=4 * width * columns + 4 * rows * columns,
            transcendentals=0,
        ),
        name="partial_sums",
    )(states, gate_codes, gate_scales, up_codes, up_scales)


def fetch_kernel(codes, scales, out, code_buf, scale_buf, sem):
    depth = 2 * BLOCK
    count = codes.shape[0] // depth

    def copy(n):
        at = pl.ds(n * depth, depth)
        return pltpu.make_async_copy(codes.at[at, :], code_buf.at[at, :], sem.at[n])

    copy_scales = pltpu.make_async_copy(scales, scale_buf, sem.at[count])
    copy_scales.start()
    for n in range(count):
        copy(n).start()
    copy_scales.wait()
    for n in range(count):
        copy(n).wait()
        at = slice(n * depth, (n + 1) * depth)
        out[at, :] = weights(code_buf[at, :], scale_buf[2 * n : 2 * n + 2, :])


def fetched_weights(codes, scales):
    anywhere = pl.BlockSpec(memory_space=pl.ANY)
    return pl.pallas_call(
        fetch_kernel,
        out_shape=jax.ShapeDtypeStruct(codes.shape, jnp.bfloat16),
        in_specs=[anywhere, anywhere],
        out_specs=pl.BlockSpec(memory_space=pltpu.VMEM),
        scratch_shapes=[
            pltpu.VMEM(codes.shape, codes.dtype),
            pltpu.VMEM(scales.shape, scales.dtype),
            pltpu.SemaphoreType.DMA((codes.shape[0] // BLOCK // 2 + 1,)),
        ],
        compiler_params=pltpu.CompilerParams(vmem_limit_bytes=16 * 1024 * 1024),
        cost_estimate=pl.CostEstimate(flops=codes.size, bytes_accessed=2 * codes.size, transcendentals=0),
        name="fetched_weights",
    )(codes, scales)


def down_kernel(piece, *rest):
    parts, (down_w, mine, theirs, act) = rest[:4], rest[4:]
    place = places()
    for (a, b, count), part in zip(PARTS, parts):
        for k in range(count):
            block = lax.rem(place[0] + a, SIDE) * SIDE + lax.rem(place[1] + b + k, SIDE)
            swap = lax.rem(lax.div(block, 2 * SIDE) + place[3], 2)
            ahead = lax.rem(lax.div(lax.rem(block, 2 * SIDE), 2) + SIDE - place[2], SIDE)
            at = (swap * SIDE + ahead) * 2 + lax.rem(block, 2)
            act[pl.ds(pl.multiple_of(at * piece, piece), piece), :] = part[k * piece : (k + 1) * piece, :]
    width = down_w.shape[1]
    half = act.shape[0] // 2
    for at in range(0, width, DOWN_TILE):
        tile = slice(at, at + DOWN_TILE)
        out = jnp.dot(act[...], down_w[:, tile], preferred_element_type=jnp.float32)
        out = out.astype(jnp.bfloat16)
        theirs[:, :, tile] = out[half:].reshape(SIDE, half // SIDE, DOWN_TILE)
        mine[:, :, tile] = out[:half].reshape(SIDE, half // SIDE, DOWN_TILE)


def down_sums(parts, down_w):
    depth, width = down_w.shape
    rows = sum(p.shape[0] for p in parts)
    piece = rows // (SIDE * SIDE)
    vmem = pl.BlockSpec(memory_space=pltpu.VMEM)
    shape = jax.ShapeDtypeStruct((SIDE, rows // 2 // SIDE, width), jnp.bfloat16)
    return pl.pallas_call(
        functools.partial(down_kernel, piece),
        out_shape=(shape, shape),
        in_specs=[vmem] * 5,
        out_specs=(vmem, vmem),
        scratch_shapes=[pltpu.VMEM((rows, depth), jnp.bfloat16)],
        compiler_params=pltpu.CompilerParams(vmem_limit_bytes=24 * 1024 * 1024),
        cost_estimate=pl.CostEstimate(
            flops=2 * rows * depth * width, bytes_accessed=2 * (depth * width + rows * depth), transcendentals=0
        ),
        name="down_sums",
    )(*parts, down_w)


def sent_along_second(parts):
    return total(parts[0], hop(parts[1], 1, 1), hop(parts[3], 1, -1), hop(parts[2], 1, 2))


def body(states, gate_codes, gate_scales, up_codes, up_scales, down_codes, down_scales):
    rows, width = states.shape
    columns = gate_codes.shape[1]
    core = lax.axis_index("core")
    iz = lax.axis_index("z")
    piece = rows // (SIDE * SIDE)

    sums = functools.partial(partial_sums, states=states, gate_codes=gate_codes)
    sums = functools.partial(sums, gate_scales=gate_scales, up_codes=up_codes, up_scales=up_scales)
    top2, low2 = sums(((2, 0), (2, 1)), (1, 1))
    passed_low, passed_top = hop(low2, 0, 1), hop(top2, 0, -1)
    top1, low1, top3, low3, own = sums(((1, 0), (1, 1), (3, 0), (3, 1), (0, 0), (0, 1)), (1, 1, 1, 1, 2))
    plus = jnp.concatenate([top1, rounded(low1, passed_low)], 0)
    minus = jnp.concatenate([rounded(top3, passed_top), low3], 0)
    plus, minus = hop(plus, 0, 1), hop(minus, 0, -1)
    line = rounded(own, plus, minus)
    line = [line[k * piece : (k + 1) * piece] for k in range(SIDE)]
    both = sent_along_second(line)
    gate, up = both[:, :columns], both[:, columns:]
    act = (jax.nn.silu(gate) * up).astype(jnp.bfloat16)

    line = jnp.concatenate([act, hop(act, 1, -1), hop(act, 1, 2), hop(act, 1, 1)], 0)
    residual = lax.dynamic_slice_in_dim(states, core * (rows // 2) + iz * (rows // 8), rows // 8, 0)
    line, residual, down_codes, down_scales = lax.optimization_barrier((line, residual, down_codes, down_scales))
    down_w = fetched_weights(down_codes, down_scales)
    parts = (line, hop(line, 0, -1), hop(line, 0, 2), hop(line, 0, 1))

    mine, theirs = down_sums(parts, down_w)
    both = rounded(mine, other_core(theirs))
    half = rows // 2
    share = half // SIDE
    got = total(both[0], hop_z(both[1], 1), hop_z(both[3], -1), hop_z(both[2], 2))
    done = lax.optimization_barrier(rounded(got, residual))
    mine = jnp.stack([done, hop_z(done, -1), hop_z(done, 2), hop_z(done, 1)])
    theirs = other_core(mine)
    out = jnp.zeros((2, SIDE, share, width), jnp.bfloat16)
    for k in range(SIDE):
        out = lax.dynamic_update_slice(out, mine[k][None, None], (core, (iz + k) % SIDE, 0, 0))
    for k in range(SIDE):
        out = lax.dynamic_update_slice(out, theirs[k][None, None], (1 - core, (iz + k) % SIDE, 0, 0))
    return out.reshape(rows, width)


def solution(mesh):
    grid = Mesh(mesh.devices.reshape(SIDE, SIDE, SIDE, 2), ("y", "x", "z", "core"))
    mp, hidden = ("y", "x"), ("z", "core")
    in_specs = (
        P(None, mp),
        P(mp, hidden),
        P(mp, hidden),
        P(mp, hidden),
        P(mp, hidden),
        P(hidden, mp),
        P(hidden, mp),
    )
    return jax.shard_map(body, mesh=grid, in_specs=in_specs, out_specs=P(None, mp), check_vma=False)
```

```python
import functools

import jax
import jax.numpy as jnp
from jax import lax
from jax.experimental import pallas as pl
from jax.experimental.pallas import tpu as pltpu
from jax.sharding import Mesh, PartitionSpec as P

BLOCK = 128
SIDE = 4
TILES = (512, 896, 896, 1024)
DEPTH = 2
DOWN_TILE = 512
PARTS = ((0, 0, 4), (1, 0, 4), (2, 0, 4), (3, 0, 4))
PLANE = ("y", "x", "core")


def hop(array, which, shift):
    pairs = []
    for y in range(SIDE):
        for x in range(SIDE):
            for c in range(2):
                if (c + which) % 2 == 0:
                    to = (y, (x + shift) % SIDE)
                else:
                    to = ((y + shift) % SIDE, x)
                pairs.append(((y * SIDE + x) * 2 + c, (to[0] * SIDE + to[1]) * 2 + c))
    return lax.ppermute(array, PLANE, pairs)


def hop_z(array, shift):
    return lax.ppermute(array, "z", [(i, (i + shift) % SIDE) for i in range(SIDE)])


def other_core(array):
    return lax.ppermute(array, "core", [(0, 1), (1, 0)])


def total(*terms):
    out = terms[0].astype(jnp.float32)
    for t in terms[1:]:
        out = out + t.astype(jnp.float32)
    return out


def rounded(*terms):
    return total(*terms).astype(jnp.bfloat16)


def weights(codes, scales):
    depth, columns = codes.shape
    groups = depth // BLOCK
    blocks = codes.astype(jnp.float32).reshape(groups, BLOCK, columns)
    return (blocks * scales[:, None, :]).reshape(depth, columns).astype(jnp.bfloat16)


def places():
    x, y, z, core = (lax.axis_index(name) for name in ("x", "y", "z", "core"))
    return jnp.where(core == 0, x, y), jnp.where(core == 0, y, x), z, core


def up_kernel(piece, halves, ends, states, gate_codes, gate_scales, up_codes, up_scales, *rest):
    outs, rest = rest[: len(ends)], rest[len(ends) :]
    turned, code_buf, scale_buf, out_buf, row_sem, code_sem, scale_sem, out_sem = rest
    place = places()
    columns = gate_codes.shape[1]
    size = 2 * piece
    tiles = []
    for width in TILES:
        tiles.append((sum(w for _, w in tiles), width))
    jobs = [(m, at, width) for at, width in tiles for m in range(2)]
    blocks = [(a, 2 * h + k) for a, h in halves for k in range(2)]

    def copy_codes(n):
        m, at, width = jobs[n]
        source = (gate_codes, up_codes)[m]
        return pltpu.make_async_copy(
            source.at[:, pl.ds(at, width)], code_buf.at[m, :, pl.ds(at, width)], code_sem.at[n]
        )

    def copy_rows(k):
        a, b = blocks[k]
        block = lax.rem(place[0] + a, SIDE) * SIDE + lax.rem(place[1] + b, SIDE)
        start = pl.multiple_of(block * piece, piece)
        return pltpu.make_async_copy(
            states.at[pl.ds(start, piece), :], turned.at[pl.ds(k * piece, piece), :], row_sem.at[k]
        )

    def copy_out(n, t):
        m, at, width = jobs[n]
        row = sum(ends[:t])
        return pltpu.make_async_copy(
            out_buf.at[m, pl.ds(row * size, ends[t] * size), pl.ds(at, width)],
            outs[t].at[:, pl.ds(m * columns + at, width)],
            out_sem.at[n, t],
        )

    copy_scales = [
        pltpu.make_async_copy(ref, scale_buf.at[m], scale_sem.at[m]) for m, ref in enumerate((gate_scales, up_scales))
    ]
    for k in range(len(blocks)):
        copy_rows(k).start()
    for copy in copy_scales:
        copy.start()
    for n in range(DEPTH):
        copy_codes(n).start()
    for k in range(len(blocks)):
        copy_rows(k).wait()
    for copy in copy_scales:
        copy.wait()
    for n, (m, at, width) in enumerate(jobs):
        copy_codes(n).wait()
        if n + DEPTH < len(jobs):
            copy_codes(n + DEPTH).start()
        w = weights(code_buf[m, :, at : at + width], scale_buf[m, :, at : at + width])
        part = jnp.dot(turned[...], w, preferred_element_type=jnp.float32)
        out_buf[m, :, at : at + width] = part.astype(jnp.bfloat16)
        for t in range(len(ends)):
            copy_out(n, t).start()
    for n in range(len(jobs)):
        for t in range(len(ends)):
            copy_out(n, t).wait()


def partial_sums(halves, ends, states, gate_codes, gate_scales, up_codes, up_scales):
    width = states.shape[1]
    columns = gate_codes.shape[1]
    piece = states.shape[0] // (SIDE * SIDE)
    rows = 2 * piece * len(halves)
    anywhere = pl.BlockSpec(memory_space=pl.ANY)
    return pl.pallas_call(
        functools.partial(up_kernel, piece, halves, ends),
        out_shape=tuple(jax.ShapeDtypeStruct((2 * piece * n, 2 * columns), jnp.bfloat16) for n in ends),
        in_specs=[anywhere] * 5,
        out_specs=(anywhere,) * len(ends),
        scratch_shapes=[
            pltpu.VMEM((rows, width), jnp.bfloat16),
            pltpu.VMEM((2, width, columns), jnp.bfloat16),
            pltpu.VMEM((2, *gate_scales.shape), jnp.float32),
            pltpu.VMEM((2, rows, columns), jnp.bfloat16),
            pltpu.SemaphoreType.DMA((2 * len(halves),)),
            pltpu.SemaphoreType.DMA((2 * len(TILES),)),
            pltpu.SemaphoreType.DMA((2,)),
            pltpu.SemaphoreType.DMA((2 * len(TILES), len(ends))),
        ],
        compiler_params=pltpu.CompilerParams(vmem_limit_bytes=60 * 1024 * 1024),
        cost_estimate=pl.CostEstimate(
            flops=4 * rows * width * columns,
            bytes_accessed=4 * width * columns + 4 * rows * columns,
            transcendentals=0,
        ),
        name="partial_sums",
    )(states, gate_codes, gate_scales, up_codes, up_scales)


def fetch_kernel(codes, scales, out, code_buf, scale_buf, sem):
    depth = 2 * BLOCK
    count = codes.shape[0] // depth

    def copy(n):
        at = pl.ds(n * depth, depth)
        return pltpu.make_async_copy(codes.at[at, :], code_buf.at[at, :], sem.at[n])

    copy_scales = pltpu.make_async_copy(scales, scale_buf, sem.at[count])
    copy_scales.start()
    for n in range(count):
        copy(n).start()
    copy_scales.wait()
    for n in range(count):
        copy(n).wait()
        at = slice(n * depth, (n + 1) * depth)
        out[at, :] = weights(code_buf[at, :], scale_buf[2 * n : 2 * n + 2, :])


def fetched_weights(codes, scales):
    anywhere = pl.BlockSpec(memory_space=pl.ANY)
    return pl.pallas_call(
        fetch_kernel,
        out_shape=jax.ShapeDtypeStruct(codes.shape, jnp.bfloat16),
        in_specs=[anywhere, anywhere],
        out_specs=pl.BlockSpec(memory_space=pltpu.VMEM),
        scratch_shapes=[
            pltpu.VMEM(codes.shape, codes.dtype),
            pltpu.VMEM(scales.shape, scales.dtype),
            pltpu.SemaphoreType.DMA((codes.shape[0] // BLOCK // 2 + 1,)),
        ],
        compiler_params=pltpu.CompilerParams(vmem_limit_bytes=16 * 1024 * 1024),
        cost_estimate=pl.CostEstimate(flops=codes.size, bytes_accessed=2 * codes.size, transcendentals=0),
        name="fetched_weights",
    )(codes, scales)


def down_kernel(piece, *rest):
    parts, (down_w, mine, theirs, act) = rest[:4], rest[4:]
    place = places()
    for (a, b, count), part in zip(PARTS, parts):
        for k in range(count):
            block = lax.rem(place[0] + a, SIDE) * SIDE + lax.rem(place[1] + b + k, SIDE)
            swap = lax.rem(lax.div(block, 2 * SIDE) + place[3], 2)
            ahead = lax.rem(lax.div(lax.rem(block, 2 * SIDE), 2) + SIDE - place[2], SIDE)
            at = (swap * SIDE + ahead) * 2 + lax.rem(block, 2)
            act[pl.ds(pl.multiple_of(at * piece, piece), piece), :] = part[k * piece : (k + 1) * piece, :]
    width = down_w.shape[1]
    half = act.shape[0] // 2
    for at in range(0, width, DOWN_TILE):
        tile = slice(at, at + DOWN_TILE)
        out = jnp.dot(act[...], down_w[:, tile], preferred_element_type=jnp.float32)
        out = out.astype(jnp.bfloat16)
        theirs[:, :, tile] = out[half:].reshape(SIDE, half // SIDE, DOWN_TILE)
        mine[:, :, tile] = out[:half].reshape(SIDE, half // SIDE, DOWN_TILE)


def down_sums(parts, down_w):
    depth, width = down_w.shape
    rows = sum(p.shape[0] for p in parts)
    piece = rows // (SIDE * SIDE)
    vmem = pl.BlockSpec(memory_space=pltpu.VMEM)
    shape = jax.ShapeDtypeStruct((SIDE, rows // 2 // SIDE, width), jnp.bfloat16)
    return pl.pallas_call(
        functools.partial(down_kernel, piece),
        out_shape=(shape, shape),
        in_specs=[vmem] * 5,
        out_specs=(vmem, vmem),
        scratch_shapes=[pltpu.VMEM((rows, depth), jnp.bfloat16)],
        compiler_params=pltpu.CompilerParams(vmem_limit_bytes=24 * 1024 * 1024),
        cost_estimate=pl.CostEstimate(
            flops=2 * rows * depth * width, bytes_accessed=2 * (depth * width + rows * depth), transcendentals=0
        ),
        name="down_sums",
    )(*parts, down_w)


def sent_along_second(parts):
    return total(parts[0], hop(parts[1], 1, 1), hop(parts[3], 1, -1), hop(parts[2], 1, 2))


def body(states, gate_codes, gate_scales, up_codes, up_scales, down_codes, down_scales):
    rows, width = states.shape
    columns = gate_codes.shape[1]
    core = lax.axis_index("core")
    iz = lax.axis_index("z")
    piece = rows // (SIDE * SIDE)

    sums = functools.partial(partial_sums, states=states, gate_codes=gate_codes)
    sums = functools.partial(sums, gate_scales=gate_scales, up_codes=up_codes, up_scales=up_scales)
    top2, low2, top1, low3 = sums(((2, 0), (2, 1), (1, 0), (3, 1)), (1, 1, 1, 1))
    passed_low, passed_top = hop(low2, 0, 1), hop(top2, 0, -1)
    straight_top, straight_low = hop(top1, 0, 1), hop(low3, 0, -1)
    low1, top3, own = sums(((1, 1), (3, 0), (0, 0), (0, 1)), (1, 1, 2))
    low = hop(rounded(low1, passed_low), 0, 1)
    top = hop(rounded(top3, passed_top), 0, -1)
    half = own.shape[0] // 2
    line = rounded(own[:half], straight_top, top), rounded(own[half:], low, straight_low)
    line = [part[k * piece : (k + 1) * piece] for part in line for k in range(2)]
    both = sent_along_second(line)
    gate, up = both[:, :columns], both[:, columns:]
    act = (jax.nn.silu(gate) * up).astype(jnp.bfloat16)

    line = jnp.concatenate([act, hop(act, 1, -1), hop(act, 1, 2), hop(act, 1, 1)], 0)
    residual = lax.dynamic_slice_in_dim(states, core * (rows // 2) + iz * (rows // 8), rows // 8, 0)
    line, residual, down_codes, down_scales = lax.optimization_barrier((line, residual, down_codes, down_scales))
    down_w = fetched_weights(down_codes, down_scales)
    parts = (line, hop(line, 0, -1), hop(line, 0, 2), hop(line, 0, 1))

    mine, theirs = down_sums(parts, down_w)
    both = rounded(mine, other_core(theirs))
    half = rows // 2
    share = half // SIDE
    got = total(both[0], hop_z(both[1], 1), hop_z(both[3], -1), hop_z(both[2], 2))
    done = lax.optimization_barrier(rounded(got, residual))
    mine = [done, hop_z(done, -1), hop_z(done, 2), hop_z(done, 1)]
    theirs = [other_core(part) for part in mine]
    out = jnp.zeros((2, SIDE, share, width), jnp.bfloat16)
    for k in range(SIDE):
        out = lax.dynamic_update_slice(out, mine[k][None, None], (core, (iz + k) % SIDE, 0, 0))
    for k in range(SIDE):
        out = lax.dynamic_update_slice(out, theirs[k][None, None], (1 - core, (iz + k) % SIDE, 0, 0))
    return out.reshape(rows, width)


def solution(mesh):
    grid = Mesh(mesh.devices.reshape(SIDE, SIDE, SIDE, 2), ("y", "x", "z", "core"))
    mp, hidden = ("y", "x"), ("z", "core")
    in_specs = (
        P(None, mp),
        P(mp, hidden),
        P(mp, hidden),
        P(mp, hidden),
        P(mp, hidden),
        P(hidden, mp),
        P(hidden, mp),
    )
    return jax.shard_map(body, mesh=grid, in_specs=in_specs, out_specs=P(None, mp), check_vma=False)
```

```python
import functools

import jax
import jax.numpy as jnp
from jax import lax
from jax.experimental import pallas as pl
from jax.experimental.pallas import tpu as pltpu
from jax.sharding import Mesh, PartitionSpec as P

BLOCK = 128
SIDE = 4
TILES = (512, 896, 896, 1024)
DEPTH = 3
DOWN_TILE = 512
PARTS = ((0, 0, 4), (1, 0, 4), (2, 0, 2), (2, 2, 2), (3, 0, 4))
PLANE = ("y", "x", "core")


def hop(array, which, shift):
    pairs = []
    for y in range(SIDE):
        for x in range(SIDE):
            for c in range(2):
                if (c + which) % 2 == 0:
                    to = (y, (x + shift) % SIDE)
                else:
                    to = ((y + shift) % SIDE, x)
                pairs.append(((y * SIDE + x) * 2 + c, (to[0] * SIDE + to[1]) * 2 + c))
    return lax.ppermute(array, PLANE, pairs)


def hop_z(array, shift):
    return lax.ppermute(array, "z", [(i, (i + shift) % SIDE) for i in range(SIDE)])


def other_core(array):
    return lax.ppermute(array, "core", [(0, 1), (1, 0)])


def total(*terms):
    out = terms[0].astype(jnp.float32)
    for t in terms[1:]:
        out = out + t.astype(jnp.float32)
    return out


def rounded(*terms):
    return total(*terms).astype(jnp.bfloat16)


def weights(codes, scales):
    depth, columns = codes.shape
    groups = depth // BLOCK
    blocks = codes.astype(jnp.float32).reshape(groups, BLOCK, columns)
    return (blocks * scales[:, None, :]).reshape(depth, columns).astype(jnp.bfloat16)


def places():
    x, y, z, core = (lax.axis_index(name) for name in ("x", "y", "z", "core"))
    return jnp.where(core == 0, x, y), jnp.where(core == 0, y, x), z, core


def up_kernel(piece, halves, ends, states, gate_codes, gate_scales, up_codes, up_scales, *rest):
    outs, rest = rest[: len(ends)], rest[len(ends) :]
    turned, code_buf, scale_buf, out_buf, row_sem, code_sem, scale_sem, out_sem = rest
    place = places()
    columns = gate_codes.shape[1]
    size = 2 * piece
    tiles = []
    for width in TILES:
        tiles.append((sum(w for _, w in tiles), width))
    jobs = [(m, at, width) for at, width in tiles for m in range(2)]
    blocks = [(a, 2 * h + k) for a, h in halves for k in range(2)]

    def copy_codes(n):
        m, at, width = jobs[n]
        source = (gate_codes, up_codes)[m]
        return pltpu.make_async_copy(
            source.at[:, pl.ds(at, width)], code_buf.at[m, :, pl.ds(at, width)], code_sem.at[n]
        )

    def copy_rows(k):
        a, b = blocks[k]
        block = lax.rem(place[0] + a, SIDE) * SIDE + lax.rem(place[1] + b, SIDE)
        start = pl.multiple_of(block * piece, piece)
        return pltpu.make_async_copy(
            states.at[pl.ds(start, piece), :], turned.at[pl.ds(k * piece, piece), :], row_sem.at[k]
        )

    def copy_out(n, t):
        m, at, width = jobs[n]
        row = sum(ends[:t])
        return pltpu.make_async_copy(
            out_buf.at[m, pl.ds(row * size, ends[t] * size), pl.ds(at, width)],
            outs[t].at[:, pl.ds(m * columns + at, width)],
            out_sem.at[n, t],
        )

    copy_scales = [
        pltpu.make_async_copy(ref, scale_buf.at[m], scale_sem.at[m]) for m, ref in enumerate((gate_scales, up_scales))
    ]
    for k in range(len(blocks)):
        copy_rows(k).start()
    for copy in copy_scales:
        copy.start()
    for n in range(DEPTH):
        copy_codes(n).start()
    for k in range(len(blocks)):
        copy_rows(k).wait()
    for copy in copy_scales:
        copy.wait()
    for n, (m, at, width) in enumerate(jobs):
        copy_codes(n).wait()
        if n + DEPTH < len(jobs):
            copy_codes(n + DEPTH).start()
        w = weights(code_buf[m, :, at : at + width], scale_buf[m, :, at : at + width])
        part = jnp.dot(turned[...], w, preferred_element_type=jnp.float32)
        out_buf[m, :, at : at + width] = part.astype(jnp.bfloat16)
        for t in range(len(ends)):
            copy_out(n, t).start()
    for n in range(len(jobs)):
        for t in range(len(ends)):
            copy_out(n, t).wait()


def partial_sums(halves, ends, states, gate_codes, gate_scales, up_codes, up_scales):
    width = states.shape[1]
    columns = gate_codes.shape[1]
    piece = states.shape[0] // (SIDE * SIDE)
    rows = 2 * piece * len(halves)
    anywhere = pl.BlockSpec(memory_space=pl.ANY)
    return pl.pallas_call(
        functools.partial(up_kernel, piece, halves, ends),
        out_shape=tuple(jax.ShapeDtypeStruct((2 * piece * n, 2 * columns), jnp.bfloat16) for n in ends),
        in_specs=[anywhere] * 5,
        out_specs=(anywhere,) * len(ends),
        scratch_shapes=[
            pltpu.VMEM((rows, width), jnp.bfloat16),
            pltpu.VMEM((2, width, columns), jnp.bfloat16),
            pltpu.VMEM((2, *gate_scales.shape), jnp.float32),
            pltpu.VMEM((2, rows, columns), jnp.bfloat16),
            pltpu.SemaphoreType.DMA((2 * len(halves),)),
            pltpu.SemaphoreType.DMA((2 * len(TILES),)),
            pltpu.SemaphoreType.DMA((2,)),
            pltpu.SemaphoreType.DMA((2 * len(TILES), len(ends))),
        ],
        compiler_params=pltpu.CompilerParams(vmem_limit_bytes=60 * 1024 * 1024),
        cost_estimate=pl.CostEstimate(
            flops=4 * rows * width * columns,
            bytes_accessed=4 * width * columns + 4 * rows * columns,
            transcendentals=0,
        ),
        name="partial_sums",
    )(states, gate_codes, gate_scales, up_codes, up_scales)


def fetch_kernel(codes, scales, out, code_buf, scale_buf, sem):
    depth = 2 * BLOCK
    count = codes.shape[0] // depth

    def copy(n):
        at = pl.ds(n * depth, depth)
        return pltpu.make_async_copy(codes.at[at, :], code_buf.at[at, :], sem.at[n])

    copy_scales = pltpu.make_async_copy(scales, scale_buf, sem.at[count])
    copy_scales.start()
    for n in range(count):
        copy(n).start()
    copy_scales.wait()
    for n in range(count):
        copy(n).wait()
        at = slice(n * depth, (n + 1) * depth)
        out[at, :] = weights(code_buf[at, :], scale_buf[2 * n : 2 * n + 2, :])


def fetched_weights(codes, scales):
    anywhere = pl.BlockSpec(memory_space=pl.ANY)
    return pl.pallas_call(
        fetch_kernel,
        out_shape=jax.ShapeDtypeStruct(codes.shape, jnp.bfloat16),
        in_specs=[anywhere, anywhere],
        out_specs=pl.BlockSpec(memory_space=pltpu.VMEM),
        scratch_shapes=[
            pltpu.VMEM(codes.shape, codes.dtype),
            pltpu.VMEM(scales.shape, scales.dtype),
            pltpu.SemaphoreType.DMA((codes.shape[0] // BLOCK // 2 + 1,)),
        ],
        compiler_params=pltpu.CompilerParams(vmem_limit_bytes=16 * 1024 * 1024),
        cost_estimate=pl.CostEstimate(flops=codes.size, bytes_accessed=2 * codes.size, transcendentals=0),
        name="fetched_weights",
    )(codes, scales)


def down_kernel(piece, *rest):
    parts, (down_w, mine, theirs, act) = rest[:5], rest[5:]
    place = places()
    for (a, b, count), part in zip(PARTS, parts):
        for k in range(count):
            block = lax.rem(place[0] + a, SIDE) * SIDE + lax.rem(place[1] + b + k, SIDE)
            swap = lax.rem(lax.div(block, 2 * SIDE) + place[3], 2)
            ahead = lax.rem(lax.div(lax.rem(block, 2 * SIDE), 2) + SIDE - place[2], SIDE)
            at = (swap * SIDE + ahead) * 2 + lax.rem(block, 2)
            act[pl.ds(pl.multiple_of(at * piece, piece), piece), :] = part[k * piece : (k + 1) * piece, :]
    width = down_w.shape[1]
    half = act.shape[0] // 2
    for at in range(0, width, DOWN_TILE):
        tile = slice(at, at + DOWN_TILE)
        out = jnp.dot(act[...], down_w[:, tile], preferred_element_type=jnp.float32)
        out = out.astype(jnp.bfloat16)
        theirs[:, :, tile] = out[half:].reshape(SIDE, half // SIDE, DOWN_TILE)
        mine[:, :, tile] = out[:half].reshape(SIDE, half // SIDE, DOWN_TILE)


def down_sums(parts, down_w):
    depth, width = down_w.shape
    rows = sum(p.shape[0] for p in parts)
    piece = rows // (SIDE * SIDE)
    vmem = pl.BlockSpec(memory_space=pltpu.VMEM)
    shape = jax.ShapeDtypeStruct((SIDE, rows // 2 // SIDE, width), jnp.bfloat16)
    return pl.pallas_call(
        functools.partial(down_kernel, piece),
        out_shape=(shape, shape),
        in_specs=[vmem] * 6,
        out_specs=(vmem, vmem),
        scratch_shapes=[pltpu.VMEM((rows, depth), jnp.bfloat16)],
        compiler_params=pltpu.CompilerParams(vmem_limit_bytes=24 * 1024 * 1024),
        cost_estimate=pl.CostEstimate(
            flops=2 * rows * depth * width, bytes_accessed=2 * (depth * width + rows * depth), transcendentals=0
        ),
        name="down_sums",
    )(*parts, down_w)


def sent_along_second(parts):
    return total(parts[0], hop(parts[1], 1, 1), hop(parts[3], 1, -1), hop(parts[2], 1, 2))


def body(states, gate_codes, gate_scales, up_codes, up_scales, down_codes, down_scales):
    rows, width = states.shape
    columns = gate_codes.shape[1]
    core = lax.axis_index("core")
    iz = lax.axis_index("z")
    piece = rows // (SIDE * SIDE)

    sums = functools.partial(partial_sums, states=states, gate_codes=gate_codes)
    sums = functools.partial(sums, gate_scales=gate_scales, up_codes=up_codes, up_scales=up_scales)
    top2, low2, top1, low3 = sums(((2, 0), (2, 1), (1, 0), (3, 1)), (1, 1, 1, 1))
    passed_low, passed_top = hop(low2, 0, 1), hop(top2, 0, -1)
    straight_top, straight_low = hop(top1, 0, 1), hop(low3, 0, -1)
    low1, top3, own = sums(((1, 1), (3, 0), (0, 0), (0, 1)), (1, 1, 2))
    low = hop(rounded(low1, passed_low), 0, 1)
    top = hop(rounded(top3, passed_top), 0, -1)
    half = own.shape[0] // 2
    line = rounded(own[:half], straight_top, top), rounded(own[half:], low, straight_low)
    line = [part[k * piece : (k + 1) * piece] for part in line for k in range(2)]
    both = sent_along_second(line)
    gate, up = both[:, :columns], both[:, columns:]
    act = (jax.nn.silu(gate) * up).astype(jnp.bfloat16)

    line = jnp.concatenate([act, hop(act, 1, -1), hop(act, 1, 2), hop(act, 1, 1)], 0)
    residual = lax.dynamic_slice_in_dim(states, core * (rows // 2) + iz * (rows // 8), rows // 8, 0)
    line, residual, down_codes, down_scales = lax.optimization_barrier((line, residual, down_codes, down_scales))
    down_w = fetched_weights(down_codes, down_scales)
    ahead, behind = hop(line, 0, -1), hop(line, 0, 1)
    ahead, behind, down_w = lax.optimization_barrier((ahead, behind, down_w))
    half = 2 * piece
    parts = (line, ahead, hop(ahead[:half], 0, -1), hop(behind[half:], 0, 1), behind)

    mine, theirs = down_sums(parts, down_w)
    both = rounded(mine, other_core(theirs))
    half = rows // 2
    share = half // SIDE
    got = total(both[0], hop_z(both[1], 1), hop_z(both[3], -1), hop_z(both[2], 2))
    done = lax.optimization_barrier(rounded(got, residual))
    mine = [done, hop_z(done, -1), hop_z(done, 2), hop_z(done, 1)]
    theirs = [other_core(part) for part in mine]
    out = jnp.zeros((2, SIDE, share, width), jnp.bfloat16)
    for k in range(SIDE):
        out = lax.dynamic_update_slice(out, mine[k][None, None], (core, (iz + k) % SIDE, 0, 0))
    for k in range(SIDE):
        out = lax.dynamic_update_slice(out, theirs[k][None, None], (1 - core, (iz + k) % SIDE, 0, 0))
    return out.reshape(rows, width)


def solution(mesh):
    grid = Mesh(mesh.devices.reshape(SIDE, SIDE, SIDE, 2), ("y", "x", "z", "core"))
    mp, hidden = ("y", "x"), ("z", "core")
    in_specs = (
        P(None, mp),
        P(mp, hidden),
        P(mp, hidden),
        P(mp, hidden),
        P(mp, hidden),
        P(hidden, mp),
        P(hidden, mp),
    )
    return jax.shard_map(body, mesh=grid, in_specs=in_specs, out_specs=P(None, mp), check_vma=False)
```
